512 devices in a mesh: kp: 32 (over z, x_hi), kz: 16 (over y, x_lo, core).
Axes of the slice: x: 4 (x_hi: 2, x_lo: 2; x = x_hi * 2 + x_lo), y: 4, z: 16, core: 2. Of those that a mesh axis runs over, the one named last changes fastest.
Arguments:
- orbitals: bfloat16 [32, 16, 2, 64, 1024], P('kp', 'kz'), may hold values from -0.75 to 0.75
- trial_vectors: bfloat16 [32, 16, 2, 2, 1024], P('kp', 'kz'), may hold values from -6 to 6
- screened_table: bfloat16 [256, 2, 1024, 1024], P('kp', None, 'kz'), may hold values from -0.09375 to 0.09375
- shift_inplane: int32 [2], replicated, may hold values from -128 to 127
- shift_depth: int32 [2], replicated, may hold values from -64 to 63
- table_entry: int32 [2], replicated, may hold values from 0 to 255
Outputs:
- kernel_image: float32 [32, 16, 2, 2, 1024], P('kp', 'kz')
The draws below stay inside these ranges and needn't reach their ends.
All inputs are finite; a program needn't handle non-finite values.
Results may differ from the reference program's by a relative error of at most 0.0049.
Values may be sent and summed in bfloat16 or wider, within the bound.
A program may use at most 64 MiB of HBM per device.

```python
import jax
import jax.numpy as jnp
from jax import lax

NMU = 1024
NV = 32
NC = 32
NTV = 2
NB = 64
KP = 32
KZ = 16
NWQ = 256


def steps_of(own_key, shape, pieces, smallest, high):
    def one(position, blocks):
        steps = jax.random.uniform(jax.random.fold_in(jax.random.fold_in(own_key, 6), position), (blocks,), jnp.float32, smallest / len(pieces), high / len(pieces))
        return jnp.repeat(jnp.exp(steps), shape[position] // blocks).reshape((-1,) + (1,) * (len(shape) - position - 1))

    level = one(*pieces[0])
    for cut in pieces[1:]:
        level = level * one(*cut)
    return level


def centred(key, shape, spread, reach, shards=(), kind=jnp.bfloat16):
    gain = steps_of(key, shape, shards, -0.22, 0.18) if shards else 1.0
    values = jax.random.normal(key, shape, jnp.float32) * spread * gain
    return jnp.minimum(jnp.maximum(values, -reach), reach).astype(kind)


def setup_inputs(seed: int = 0) -> dict:
    seeds = jax.random.split(jax.random.key(seed), 7)
    return {
        "orbitals": centred(seeds[0], (KP, KZ, 2, NB, NMU), 0.125, 0.75, ((0, 32), (1, 16))),
        "trial_vectors": centred(seeds[1], (KP, KZ, NTV, 2, NC * NV), 1.0, 6.0, ((0, 32), (1, 16))),
        "screened_table": centred(seeds[2], (NWQ, 2, NMU, NMU), 0.015625, 0.09375, ((0, 32), (2, 16))),
        "shift_inplane": jax.random.randint(seeds[3], (2,), -4 * KP, 4 * KP).astype(jnp.int32),
        "shift_depth": jax.random.randint(seeds[4], (2,), -4 * KZ, 4 * KZ).astype(jnp.int32),
        "table_entry": jax.random.randint(seeds[5], (2,), 0, NWQ).astype(jnp.int32),
    }


def pair_term(own_valence, own_conduction, next_valence, next_conduction, next_trial, screen_rows):
    valence_count = own_valence.shape[1]
    conduction_count = own_conduction.shape[1]
    row_span = own_conduction.shape[2]
    points = own_valence.shape[2]
    vector_count = next_trial.shape[0]
    trial_matrix = next_trial.reshape(vector_count, 2, conduction_count, valence_count)
    real_part = jnp.swapaxes(trial_matrix[:, 0], 1, 2)
    imag_part = jnp.swapaxes(trial_matrix[:, 1], 1, 2)
    upper_rows = jnp.concatenate([real_part, -imag_part], axis=2)
    lower_rows = jnp.concatenate([imag_part, real_part], axis=2)
    coeffs = jnp.stack([upper_rows, lower_rows], axis=1).reshape(vector_count * 2 * valence_count, 2 * conduction_count)
    amplitude = jnp.dot(coeffs, next_conduction.reshape(2 * conduction_count, row_span), preferred_element_type=jnp.float32)
    amplitude = amplitude.astype(jnp.bfloat16).reshape(vector_count, 2, valence_count, row_span)
    partner_rows = next_valence.reshape(2 * valence_count, points)
    own_real = own_valence[0]
    own_imag = own_valence[1]
    valence_stack = jnp.concatenate([jnp.concatenate([own_real, -own_imag], axis=1), jnp.concatenate([own_imag, own_real], axis=1)], axis=0)
    block = min(512, row_span)

    def one_vector(amplitude_pair):
        amp_real = amplitude_pair[0]
        amp_imag = amplitude_pair[1]

        def add_block(block_index, accumulated):
            row_start = block_index * block
            part_real = lax.dynamic_slice_in_dim(amp_real, row_start, block, 1)
            part_imag = lax.dynamic_slice_in_dim(amp_imag, row_start, block, 1)
            left_factor = jnp.concatenate([jnp.concatenate([part_real, part_imag], axis=0), jnp.concatenate([part_imag, -part_real], axis=0)], axis=1)
            expanded = lax.dot_general(left_factor, partner_rows, (((0,), (0,)), ((), ())), preferred_element_type=jnp.float32)
            exp_real = expanded[:block]
            exp_imag = expanded[block:]
            screen_part = lax.dynamic_slice_in_dim(screen_rows, row_start, block, 1)
            w_real = screen_part[0].astype(jnp.float32)
            w_imag = screen_part[1].astype(jnp.float32)
            product = jnp.concatenate([w_real * exp_real - w_imag * exp_imag, w_real * exp_imag + w_imag * exp_real], axis=1).astype(jnp.bfloat16)
            half_product = lax.dot_general(product, valence_stack, (((1,), (1,)), ((), ())), preferred_element_type=jnp.float32).astype(jnp.bfloat16)
            half_real = half_product[:, :valence_count]
            half_imag = half_product[:, valence_count:]
            half_stack = jnp.concatenate([jnp.concatenate([half_real, half_imag], axis=1), jnp.concatenate([half_imag, -half_real], axis=1)], axis=0)
            cond_part = lax.dynamic_slice_in_dim(own_conduction, row_start, block, 2)
            cond_cat = jnp.concatenate([cond_part[0], cond_part[1]], axis=1)
            return accumulated + jnp.dot(cond_cat, half_stack, preferred_element_type=jnp.float32)

        result = lax.fori_loop(0, row_span // block, add_block, jnp.zeros((conduction_count, 2 * valence_count), jnp.float32))
        return jnp.stack([result[:, :valence_count].reshape(-1), result[:, valence_count:].reshape(-1)])

    return lax.map(one_vector, amplitude)


def reference(orbitals, trial_vectors, screened_table, shift_inplane, shift_depth, table_entry):
    plane_count = orbitals.shape[0]
    depth_count = orbitals.shape[1]

    def one_point(flat_index):
        plane_index = flat_index // depth_count
        depth_index = flat_index % depth_count
        own_orbitals = orbitals[plane_index, depth_index]
        accumulated = jnp.zeros(trial_vectors.shape[2:], jnp.float32)
        for transfer in range(2):
            plane_next = ((plane_index + shift_inplane[transfer]) % plane_count).astype(jnp.int32)
            depth_next = ((depth_index + shift_depth[transfer]) % depth_count).astype(jnp.int32)
            partner = orbitals[plane_next, depth_next]
            partner_trial = trial_vectors[plane_next, depth_next]
            screen_full = screened_table[table_entry[transfer]]
            accumulated = accumulated + pair_term(own_orbitals[:, :NV], own_orbitals[:, NV:], partner[:, :NV], partner[:, NV:], partner_trial, screen_full)
        return accumulated

    result = lax.map(one_point, jnp.arange(plane_count * depth_count, dtype=jnp.int32))
    return result.reshape(trial_vectors.shape)
```

```python
import functools

import jax
import jax.numpy as jnp
from jax import lax
from jax.experimental import pallas as pl
from jax.experimental.pallas import tpu as pltpu
from jax.sharding import PartitionSpec as P

MESH = pl.DeviceIdType.MESH
NV = 32
NZ = 16
BF = jnp.bfloat16
F32 = jnp.float32
ANY = pl.BlockSpec(memory_space=pl.ANY)
VM = pl.BlockSpec(memory_space=pltpu.VMEM)
DMA = pltpu.SemaphoreType.DMA


def coords():
    kp = lax.axis_index("kp")
    kz = lax.axis_index("kz")
    return kp // 2, (kp % 2) * 2 + (kz // 2) % 2, kz // 4, kz % 2


def dev(z, x, y, c):
    return (z * 2 + x // 2, y * 4 + (x % 2) * 2 + c)


def remote(src, dst, send, recv, target):
    return pltpu.make_async_remote_copy(
        src_ref=src, dst_ref=dst, send_sem=send, recv_sem=recv, device_id=target, device_id_type=MESH
    )


def greet(peers):
    barrier = pltpu.get_barrier_semaphore()
    for peer in peers:
        pl.semaphore_signal(barrier, inc=1, device_id=peer, device_id_type=MESH)
    pl.semaphore_wait(barrier, len(peers))


def plane_peers(z, x, y, c):
    peers = []
    for dx in range(4):
        for dc in range(2):
            if dx or dc:
                peers.append(dev(z, (x + dx) % 4, y, (c + dc) % 2))
    for dy in range(1, 4):
        for dc in range(2):
            peers.append(dev(z, x, (y + dy) % 4, (c + dc) % 2))
    return peers


REACH = {0: (6, 10, 3, 13, 1, 15), 3: (4, 2), 6: (7, 5), 10: (8, 9, 11), 13: (12, 14)}


class Spread:
    def __init__(self, owner, slab, w, sems, place):
        self.z0, self.xh0 = owner // 2, owner % 2
        self.slab, self.w, self.sems = slab, w, sems
        self.z, self.x, self.y, self.c = place
        self.r = (self.z - self.z0 + NZ) % NZ
        self.straight = self.x % 2 == self.c
        self.root = jnp.logical_and(self.z == self.z0, self.x // 2 == self.xh0)

    def columns(self, tx):
        return self.slab.at[:, :, pl.ds(pl.multiple_of(tx * 256, 256), 256)]

    def piece(self, dx):
        z, x, y, c = self.z, self.x, self.y, self.c
        tx = (x + dx) % 4
        return remote(
            self.columns(tx), self.w.at[c], self.sems["scatter"].at[dx], self.sems["recv"].at[c], dev(z, tx, y, x % 2)
        )

    def local(self):
        return pltpu.make_async_copy(self.columns(self.x), self.w.at[self.c], self.sems["recv"].at[self.c])

    def scatter(self):
        @pl.when(self.root)
        def _():
            for dx in range(1, 4):
                self.piece(dx).start()

            @pl.when(self.straight)
            def _():
                self.local().start()

            @pl.when(jnp.logical_not(self.straight))
            def _():
                self.piece(0).start()

    def link(self, i, r, to):
        z = (self.z + to - r + NZ) % NZ
        return remote(
            self.w, self.w, self.sems["out"].at[i], self.sems["whole"].at[0], dev(z, self.x, self.y, self.c)
        )

    def pass_on(self, r):
        for i, to in enumerate(REACH[r]):
            self.link(i, r, to).start()

    def start_root(self):
        @pl.when(self.r == 0)
        def _():
            for half in range(2):
                mine = jnp.logical_and(jnp.logical_and(self.x // 2 == self.xh0, self.straight), self.c == half)

                @pl.when(mine)
                def _():
                    self.local().wait()

                @pl.when(jnp.logical_not(mine))
                def _():
                    remote(
                        self.w.at[half], self.w.at[half], self.sems["scatter"].at[0], self.sems["recv"].at[half],
                        dev((self.z + 1) % NZ, self.x, self.y, self.c),
                    ).wait_recv()

            self.pass_on(0)

    def relay(self):
        for r in (3, 6, 10, 13):

            @pl.when(self.r == r)
            def _():
                self.link(0, r, REACH[r][0]).wait_recv()
                self.pass_on(r)

    def finish(self):
        hubs = (0, 3, 6, 10, 13)
        leaf = functools.reduce(jnp.logical_and, [self.r != r for r in hubs])

        @pl.when(leaf)
        def _():
            self.link(0, 0, 1).wait_recv()

        @pl.when(self.root)
        def _():
            for dx in range(1, 4):
                self.piece(dx).wait_send()

            @pl.when(jnp.logical_not(self.straight))
            def _():
                self.piece(0).wait_send()

        for r in hubs:

            @pl.when(self.r == r)
            def _():
                for i, to in enumerate(REACH[r]):
                    self.link(i, r, to).wait_send()


class Gather:
    def __init__(self, src_v, src_c, dst_v, dst_c, sems, place):
        self.sv, self.sc, self.dv, self.dc, self.s = src_v, src_c, dst_v, dst_c, sems
        self.z, self.x, self.y, self.c = place

    def vcopy(self, kind, half):
        z, x, y, c = self.z, self.x, self.y, self.c
        to_next = kind in (0, 2)
        row = y if kind < 2 else ((y + 3) % 4 if kind == 2 else (y + 1) % 4)
        target = (y + 1) % 4 if to_next else (y + 3) % 4
        block = self.dv.at[c, row, pl.ds(2 * half, 2)]
        src = self.sv.at[pl.ds(2 * half, 2)] if kind < 2 else block
        return remote(src, block, self.s["vs"].at[kind, half], self.s["vr"].at[kind, half], dev(z, x, target, c))

    def ccopy(self, kind, half):
        z, x, y, c = self.z, self.x, self.y, self.c
        to_next = kind in (0, 2)
        row = x if kind < 2 else ((x + 3) % 4 if kind == 2 else (x + 1) % 4)
        target = (x + 1) % 4 if to_next else (x + 3) % 4
        block = self.dc.at[row, pl.ds(4 * half, 4)]
        src = self.sc.at[pl.ds(4 * half, 4)] if kind < 2 else block
        return remote(src, block, self.s["cs"].at[kind, half], self.s["cr"].at[kind, half], dev(z, target, y, c))

    def twin(self, step):
        z, x, y, c = self.z, self.x, self.y, self.c
        row = (y + step) % 4
        block = self.dv.at[c, row]
        src = self.sv if step == 0 else block
        return remote(src, block, self.s["ts"].at[step], self.s["tr"].at[step], dev(z, x, y, 1 - c))

    def locals(self):
        return (
            pltpu.make_async_copy(self.sv, self.dv.at[self.c, self.y], self.s["loc"].at[0]),
            pltpu.make_async_copy(self.sc, self.dc.at[self.x], self.s["loc"].at[1]),
        )

    def start(self):
        for half in range(2):
            for kind in range(2):
                h = half if kind == 0 else 1 - half
                self.vcopy(kind, h).start()
                self.ccopy(kind, h).start()
        self.twin(0).start()
        for copy in self.locals():
            copy.start()

    def forward(self):
        self.vcopy(0, 0).wait_recv()
        self.vcopy(2, 0).start()
        self.ccopy(0, 0).wait_recv()
        self.ccopy(2, 0).start()
        self.vcopy(1, 1).wait_recv()
        self.vcopy(3, 1).start()
        self.ccopy(1, 1).wait_recv()
        self.ccopy(3, 1).start()

    def share(self):
        self.vcopy(0, 1).wait_recv()
        self.twin(3).start()
        self.vcopy(1, 0).wait_recv()
        self.twin(1).start()
        self.vcopy(2, 0).wait_recv()
        self.vcopy(3, 1).wait_recv()
        self.twin(2).start()

    def finish(self):
        self.ccopy(0, 1).wait_recv()
        self.ccopy(1, 0).wait_recv()
        self.ccopy(2, 0).wait_recv()
        self.ccopy(3, 1).wait_recv()
        for copy in self.locals():
            copy.wait()
        for step in range(4):
            self.twin(step).wait()
        for kind in range(2):
            for half in range(2):
                self.vcopy(kind, half).wait_send()
                self.ccopy(kind, half).wait_send()
        for kind, half in ((2, 0), (3, 1)):
            self.vcopy(kind, half).wait_send()
            self.ccopy(kind, half).wait_send()


GATHER_SEMS = [DMA((4, 2)), DMA((4, 2)), DMA((4, 2)), DMA((4, 2)), DMA((4,)), DMA((4,)), DMA((2,))]
GATHER_NAMES = ["vs", "vr", "cs", "cr", "ts", "tr", "loc"]
SPREAD_SEMS = [DMA((4,)), DMA((2,)), DMA((6,)), DMA((1,))]
SPREAD_NAMES = ["scatter", "recv", "out", "whole"]
NEAR = 2


def hub_peers(z, x, y, c):
    return [dev((z + d) % NZ, x, y, c) for d in (1, 2, 3, 6, 10, 13, 14, 15)]


def first_kernel(owner, vblk, cblk, slab, rv, rc, ov, oc, w, av_s, av_r, ac_s, ac_r, loc, rs, rr, *sems):
    z, x, y, c = place = coords()
    gsem = dict(zip(GATHER_NAMES, sems[: len(GATHER_NAMES)]))
    wsem = dict(zip(SPREAD_NAMES, sems[len(GATHER_NAMES) :]))
    spread = Spread(owner, slab, w, wsem, place)
    gather = Gather(rv.at[0], rc.at[0], ov, oc, gsem, place)
    greet(plane_peers(z, x, y, c) + hub_peers(z, x, y, c))
    spread.scatter()

    def va(dx):
        tx = (x + dx) % 4
        return remote(vblk.at[tx], rv.at[0, x], av_s.at[dx], av_r.at[dx], dev(z, tx, y, c))

    def ca(dy, dc):
        ty, tc = (y + dy) % 4, (c + dc) % 2
        i = dy * 2 + dc
        return remote(cblk.at[ty * 2 + tc], rc.at[0, y * 2 + c], ac_s.at[i], ac_r.at[i], dev(z, x, ty, tc))

    across = [(dy, dc) for dy in range(4) for dc in range(2) if dy or dc]
    own_v = pltpu.make_async_copy(vblk.at[x], rv.at[0, x], loc.at[0])
    own_c = pltpu.make_async_copy(cblk.at[y * 2 + c], rc.at[0, y * 2 + c], loc.at[1])
    for dx in (1, 3, 2):
        va(dx).start()
    for dy, dc in across:
        ca(dy, dc).start()
    own_v.start()
    own_c.start()
    spread.start_root()

    def hop(h, part, down):
        ref = rv if part == 0 else rc
        slots = 2 * NEAR + 1
        src = (h - 1) if down else (slots + 1 - h) % slots
        dst = h if down else slots - h
        way = 0 if down else 1
        target = dev((z + NZ - 1) % NZ if down else (z + 1) % NZ, x, y, c)
        return remote(ref.at[src], ref.at[dst], rs.at[h, part, way], rr.at[h, part, way], target)

    for dx in (1, 3, 2):
        va(dx).wait_recv()
    own_v.wait()
    hop(1, 0, True).start()
    hop(1, 0, False).start()
    for dy, dc in across:
        ca(dy, dc).wait_recv()
    own_c.wait()
    hop(1, 1, True).start()
    hop(1, 1, False).start()
    gather.start()
    for part in range(2):
        for down in (True, False):
            hop(1, part, down).wait_recv()
            hop(2, part, down).start()
    gather.forward()
    spread.relay()
    gather.share()
    gather.finish()
    for part in range(2):
        for down in (True, False):
            hop(2, part, down).wait_recv()
    spread.finish()
    for dx in (1, 3, 2):
        va(dx).wait_send()
    for dy, dc in across:
        ca(dy, dc).wait_send()
    for h in (1, 2):
        for part in range(2):
            for down in (True, False):
                hop(h, part, down).wait_send()


def ring_kernel(reach, near_v, near_c, rv, rc, rs, rr):
    z, x, y, c = coords()
    below, above = dev((z + NZ - 1) % NZ, x, y, c), dev((z + 1) % NZ, x, y, c)
    greet([below, above])
    first, middle = NEAR + 1, NZ // 2

    def hop(h, part, down, src=None):
        ref = rv if part == 0 else rc
        dst = ref.at[h - first] if down else ref.at[NZ - h - first]
        if src is None:
            src = ref.at[h - 1 - first] if down else ref.at[NZ - h + 1 - first]
        way = 0 if down else 1
        return remote(src, dst, rs.at[h, part, way], rr.at[h, part, way], below if down else above)

    for part in range(2):
        ref = near_v if part == 0 else near_c
        hop(first, part, True, ref.at[NEAR]).start()
        hop(first, part, False, ref.at[NEAR + 1]).start()

    def body(h, carry):
        for part in range(2):
            for down in (True, False):
                hop(h - 1, part, down).wait_recv()
                hop(h, part, down).start()
        return carry

    whole = min(reach, middle - 1)
    lax.fori_loop(first + 1, whole + 1, body, 0)
    for part in range(2):
        for down in (True, False):
            hop(whole, part, down).wait_recv()
        if reach == middle:
            hop(middle, part, part == 0).start()

    def done(h, carry):
        for part in range(2):
            for down in (True, False):
                hop(h, part, down).wait_send()
        return carry

    lax.fori_loop(first, whole + 1, done, 0)
    if reach == middle:
        hop(middle, 0, True).wait()
        hop(middle, 1, False).wait()


def idle_kernel(near_v, near_c, rv, rc, rs, rr):
    pass


def gather_kernel(owner, sel_v, sel_c, slab, pv, pc, w, *sems):
    z, x, y, c = place = coords()
    wsem = dict(zip(SPREAD_NAMES, sems[2 * len(GATHER_NAMES) :]))
    spread = Spread(owner, slab, w, wsem, place)
    gathers = []
    for t in range(2):
        mine = sems[t * len(GATHER_NAMES) : (t + 1) * len(GATHER_NAMES)]
        gathers.append(
            Gather(sel_v.at[t], sel_c.at[t], pv.at[t], pc.at[t], dict(zip(GATHER_NAMES, mine)), place)
        )
    greet(plane_peers(z, x, y, c) + hub_peers(z, x, y, c))
    spread.scatter()
    for g in gathers:
        g.start()
    spread.start_root()
    gathers[0].forward()
    gathers[1].forward()
    gathers[0].share()
    spread.relay()
    gathers[1].share()
    for g in gathers:
        g.finish()
    spread.finish()


def exchange_kernel(part, out, send, recv, loc):
    z, x, y, c = coords()
    me = y * 8 + x * 2 + c
    peers, copies = [], []
    for dy in range(4):
        for dx in range(4):
            for dc in range(2):
                if dx or dy or dc:
                    tx, ty, tc = (x + dx) % 4, (y + dy) % 4, (c + dc) % 2
                    i = dy * 8 + dx * 2 + dc
                    target = dev(z, tx, ty, tc)
                    peers.append(target)
                    copies.append(
                        remote(part.at[ty * 8 + tx * 2 + tc], out.at[me], send.at[i], recv.at[i], target)
                    )
    greet(peers)
    for copy in copies:
        copy.start()
    own = pltpu.make_async_copy(part.at[me], out.at[me], loc.at[0])
    own.start()
    own.wait()
    for copy in copies:
        copy.wait()


def select_kernel(slot, near_v, near_c, rv, rc, sel_v, sel_c, sem):
    waits = []

    def take(s, near, far, dst, semaphore):
        close = jnp.logical_or(s <= NEAR, s >= NZ - NEAR)

        @pl.when(close)
        def _():
            i = jnp.where(s <= NEAR, s, s - (NZ - 2 * NEAR - 1))
            pltpu.make_async_copy(near(i), dst, semaphore).start()

        @pl.when(jnp.logical_not(close))
        def _():
            pltpu.make_async_copy(far(s - NEAR - 1), dst, semaphore).start()

        waits.append(pltpu.make_async_copy(near(0), dst, semaphore))

    for t in range(2):
        for x in range(4):
            take(slot[t, x // 2], lambda i: near_v.at[i, x], lambda i: rv.at[i, x], sel_v.at[t, x], sem.at[t, x])
        take(slot[t, 2], lambda i: near_c.at[i], lambda i: rc.at[i], sel_c.at[t], sem.at[t, 4])
    for copy in waits:
        copy.wait()


def turned(a, axis_lanes):
    lane = lax.broadcasted_iota(jnp.int32, a.shape, 1)
    first = (lane // 32) % 2 == 0
    return jnp.where(first, pltpu.roll(a, axis_lanes - 32, 1), -pltpu.roll(a, 32, 1))


def compute_kernel(partner, ov, oc, pv, pc, w0, w1, out, wf):
    for t, w in enumerate((w0, w1)):
        for half in range(2):
            for part in range(2):
                wf[t, part, pl.ds(64 * half, 64)] = w[half, part].astype(F32)

    def one(k, carry):
        y, x, c = k // 8, (k // 2) % 4, k % 2
        own_v = ov[c, y, x, pl.ds(0, 64)]
        own_c = oc[x, y * 2 + c]
        swapped = jnp.concatenate([-own_v[32:], own_v[:32]], axis=0)
        stack = jnp.concatenate([own_v, swapped], axis=1)
        halves = [None, None]
        for t in range(2):
            q = partner[t, k]
            qy, qx, qc = q // 8, (q // 2) % 4, q % 2
            slab = pv[t, qc, qy, qx]
            trial = jnp.concatenate([slab[64:, :128], slab[64:, 128:]], axis=0).astype(F32)
            spun = turned(trial, 128)
            coeff = jnp.concatenate(
                [jnp.concatenate([trial, spun], axis=1), jnp.concatenate([-spun, trial], axis=1)], axis=0
            ).astype(BF)
            left = lax.dot_general(
                pc[t, qx, qy * 2 + qc], coeff, (((0,), (0,)), ((), ())), preferred_element_type=F32
            ).astype(BF)
            wr, wi = wf[t, 0], wf[t, 1]
            for n in range(2):
                rows = jnp.concatenate([left[:, 64 * n : 64 * n + 64], left[:, 128 + 64 * n : 192 + 64 * n]], axis=0)
                expanded = jnp.dot(rows, slab[:64], preferred_element_type=F32)
                a, b = expanded[:128], expanded[128:]
                s = jnp.concatenate([(wr * a - wi * b).astype(BF), (wr * b + wi * a).astype(BF)], axis=1)
                h = lax.dot_general(s, stack, (((1,), (1,)), ((), ())), preferred_element_type=F32)
                halves[n] = h if halves[n] is None else halves[n] + h
        half = jnp.concatenate([halves[0], halves[1]], axis=0).astype(BF)
        half = jnp.concatenate([half[:128], half[128:]], axis=1)
        image = jnp.dot(own_c, half, preferred_element_type=F32)
        out[k] = (image[:32] + turned(image[32:], 128)).astype(out.dtype)
        return carry

    lax.fori_loop(0, 32, one, 0, unroll=4)


def shards(orbitals, trial_vectors, screened_table, shift_inplane, shift_depth, table_entry):
    own = orbitals[0, 0]
    valence = own[:, :NV].reshape(64, 1024)
    conduction = own[:, NV:].reshape(64, 1024)
    trial = trial_vectors[0, 0].reshape(2, 2, 32, 32).transpose(2, 0, 1, 3).reshape(32, 128)
    trial = jnp.concatenate([trial[:16], trial[16:]], axis=1)
    vblk = jnp.concatenate(
        [valence.reshape(64, 4, 256).transpose(1, 0, 2), jnp.broadcast_to(trial[None], (4, 16, 256))], axis=1
    )
    cblk = conduction.reshape(64, 8, 128).transpose(1, 0, 2)
    slabs = [
        lax.dynamic_index_in_dim(screened_table, table_entry[t] % 8, 0, keepdims=False) for t in range(2)
    ]
    owners = table_entry // 8
    plane = shift_inplane % 32
    depth = shift_depth % 16
    xh = lax.axis_index("kp") % 2

    def slot_of(side):
        return (((side + plane) % 2 + plane) // 2) % NZ

    slots = jnp.stack([slot_of(0), slot_of(1), slot_of(xh)], axis=1).astype(jnp.int32)
    k = jnp.arange(32)
    ky, kx, kc = k // 8, (k // 2) % 4, k % 2
    side = (kx // 2 + plane[:, None]) % 2
    line = (ky * 4 + (kx % 2) * 2 + kc + depth[:, None]) % 16
    partner = ((line // 4) * 8 + (side * 2 + (line // 2) % 2) * 2 + line % 2).astype(jnp.int32)

    sds = jax.ShapeDtypeStruct
    wshape = sds((2, 2, 64, 256), BF)
    vshape, cshape = (2, 4, 4, 80, 256), (4, 8, 64, 128)

    near = 2 * NEAR + 1
    far = NZ - near

    def first(owner):
        return lambda v, c, s: pl.pallas_call(
            functools.partial(first_kernel, owner),
            out_shape=(
                sds((near, 4, 80, 256), BF), sds((near, 8, 64, 128), BF), sds(vshape, BF), sds(cshape, BF), wshape,
            ),
            in_specs=[VM, VM, VM],
            out_specs=(ANY,) * 5,
            scratch_shapes=[
                DMA((4,)), DMA((4,)), DMA((8,)), DMA((8,)), DMA((2,)), DMA((3, 2, 2)), DMA((3, 2, 2)),
                *GATHER_SEMS, *SPREAD_SEMS,
            ],
            compiler_params=pltpu.CompilerParams(collective_id=owner, has_side_effects=True),
            name="first",
        )(v, c, s)

    def ring(reach):
        moves = reach > NEAR
        return lambda v, c: pl.pallas_call(
            functools.partial(ring_kernel, reach) if moves else idle_kernel,
            out_shape=(sds((far, 4, 80, 256), BF), sds((far, 8, 64, 128), BF)),
            in_specs=[ANY, ANY],
            out_specs=(ANY, ANY),
            scratch_shapes=[DMA((9, 2, 2)), DMA((9, 2, 2))],
            compiler_params=pltpu.CompilerParams(
                collective_id=65 + reach if moves else None, has_side_effects=True
            ),
            name="ring",
        )(v, c)

    def gather(owner):
        return lambda v, c, s: pl.pallas_call(
            functools.partial(gather_kernel, owner),
            out_shape=(sds((2,) + vshape, BF), sds((2,) + cshape, BF), wshape),
            in_specs=[VM, VM, VM],
            out_specs=(ANY,) * 3,
            scratch_shapes=[*GATHER_SEMS, *GATHER_SEMS, *SPREAD_SEMS],
            compiler_params=pltpu.CompilerParams(collective_id=32 + owner, has_side_effects=True),
            name="gather",
        )(v, c, s)

    near_v, near_c, ov, oc, w0 = lax.switch(owners[0], [first(i) for i in range(32)], vblk, cblk, slabs[0])
    distance = jnp.max(jnp.minimum(slots[:, :2], NZ - slots[:, :2]))
    rv, rc = lax.switch(
        jnp.maximum(distance, NEAR) - NEAR, [ring(i) for i in range(NEAR, NZ // 2 + 1)], near_v, near_c
    )
    sel_v, sel_c = pl.pallas_call(
        select_kernel,
        out_shape=(sds((2, 4, 80, 256), BF), sds((2, 8, 64, 128), BF)),
        in_specs=[pl.BlockSpec(memory_space=pltpu.SMEM)] + [ANY] * 4,
        out_specs=(VM, VM),
        scratch_shapes=[DMA((2, 5))],
        name="select",
    )(slots, near_v, near_c, rv, rc)
    pv, pc, w1 = lax.switch(owners[1], [gather(i) for i in range(32)], sel_v, sel_c, slabs[1])
    partial = pl.pallas_call(
        compute_kernel,
        out_shape=sds((32, 32, 128), BF),
        in_specs=[pl.BlockSpec(memory_space=pltpu.SMEM)] + [VM] * 6,
        out_specs=VM,
        scratch_shapes=[pltpu.VMEM((2, 2, 128, 256), F32)],
        name="compute",
    )(partner, ov, oc, pv, pc, w0, w1)
    terms = pl.pallas_call(
        exchange_kernel,
        out_shape=sds((32, 32, 128), BF),
        in_specs=[VM],
        out_specs=ANY,
        scratch_shapes=[DMA((32,)), DMA((32,)), DMA((1,))],
        compiler_params=pltpu.CompilerParams(collective_id=64, has_side_effects=True),
        name="exchange",
    )(partial)
    image = jnp.sum(terms.astype(F32), axis=0)
    image = image.reshape(32, 2, 2, 32).transpose(1, 2, 0, 3).reshape(2, 2, 1024)
    return image[None, None]


def solution(mesh):
    in_specs = (
        P("kp", "kz", None, None, None),
        P("kp", "kz", None, None, None),
        P("kp", None, "kz", None),
        P(),
        P(),
        P(),
    )
    out_specs = P("kp", "kz", None, None, None)
    return jax.shard_map(shards, mesh=mesh, in_specs=in_specs, out_specs=out_specs, check_vma=False)
```
